32 devices in a mesh: row: 4 (over y, core), col: 8 (over z, x).
Axes of the slice: x: 2, y: 2, z: 4, core: 2. Of those that a mesh axis runs over, the one named last changes fastest.
Arguments:
- matrix: float32 [32768, 1024], P('row', 'col'), may hold values from -700 to 700, as said below
Outputs:
- r_rows: float32 [2, 128, 1024], P(None, None, 'col')
- factored: float32 [32768, 1024], P('row', 'col')
The draws below stay inside these ranges and needn't reach their ends.
Inputs may be any that keep to these rules, and one draw needn't show every extreme that they name: `matrix`: real-valued entries.
All inputs are finite; a program needn't handle non-finite values.
Results may differ from the reference program's by a relative error of at most 0.0003.
Values sent between devices are 32-bit elements; how exact they have to be, the bound alone decides.
A program may use at most 64 MiB of HBM per device.

```python
import math
import jax
import jax.numpy as jnp
from jax import lax

B = 128
ROWS = 32768
NCOL = 1024


def draw_matrix(key, part):
    keys = jax.random.split(key, 4)
    shared = jnp.clip(jax.random.normal(keys[0], (ROWS, B), jnp.float32), -4.0, 4.0)
    noise_part = jnp.clip(jax.random.normal(keys[1], (ROWS, NCOL), jnp.float32), -4.0, 4.0)
    row_spread = jnp.exp(jax.random.uniform(keys[3], (ROWS, 1), jnp.float32, 0.0, math.log(10.0)))
    weights = jnp.exp(jax.random.uniform(keys[2], (1, NCOL), jnp.float32, math.log(0.5), math.log(2.0)))
    tiled = jnp.tile(shared, (1, NCOL // B))
    row_ids = jnp.arange(ROWS, dtype=jnp.int32)[:, None]
    col_ids = jnp.arange(NCOL, dtype=jnp.int32)[None, :]
    planted = jnp.where((row_ids + 37 * (col_ids // B)) % B == col_ids % B, 2.0, 0.0).astype(jnp.float32)
    ramp = 1.0 + 2.0 * jnp.arange(ROWS, dtype=jnp.float32)[:, None] / (ROWS - 1)
    return (row_spread * ramp * (weights * tiled + noise_part + planted)).astype(jnp.float32)


def setup_inputs(seed: int = 0) -> dict:
    splits = jax.random.split(jax.random.key(seed), 2)
    matrix = draw_matrix(jax.random.fold_in(splits[1], 71), 0)
    return dict(matrix=matrix)


def gram_matrix(block):
    return lax.dot_general(block, block, (((0,), (0,)), ((), ())), precision=lax.Precision.HIGHEST)

def reference(matrix):
    factor_scale = math.sqrt(ROWS)
    working = matrix
    couplings = []
    first_basis = None
    for panel_id in range(2):
        panel_rows = working[:, panel_id * B:(panel_id + 1) * B]
        lower_factor = jnp.linalg.cholesky(gram_matrix(panel_rows))
        inverse_lower = jax.scipy.linalg.solve_triangular(lower_factor, jnp.eye(B, dtype=jnp.float32), lower=True)
        basis_rows = lax.dot_general(panel_rows, inverse_lower, (((1,), (1,)), ((), ())), precision=lax.Precision.HIGHEST)
        cross_rows = lax.dot_general(basis_rows, working, (((0,), (0,)), ((), ())), precision=lax.Precision.HIGHEST)
        working = working - jnp.dot(basis_rows, cross_rows, precision=lax.Precision.HIGHEST)
        scaled_basis = factor_scale * basis_rows
        working = working.at[:, panel_id * B:(panel_id + 1) * B].set(scaled_basis)
        if panel_id == 0:
            first_basis = scaled_basis
        couplings.append(cross_rows / factor_scale)
    working = working.at[:, 0:B].set(first_basis)
    return (jnp.stack(couplings), working)
```

```python
import functools
import math

import jax
import jax.numpy as jnp
from jax import lax
from jax.experimental import pallas as pl
from jax.experimental.pallas import tpu as pltpu
from jax.sharding import PartitionSpec as P

MESH = pl.DeviceIdType.MESH
HIGHEST = lax.Precision.HIGHEST
PANELS = 2
BLOCK = 32
TOGETHER = 16
TILE = 64
GROUP = 4
LAG = 8
LATE = 24
AHEAD = 16
CHUNK = 1024


def outer(a, b):
    return lax.dot_general(
        a, b, (((0,), (0,)), ((), ())), precision=HIGHEST, preferred_element_type=jnp.float32
    )


def product(a, b, over=((1,), (0,))):
    return lax.dot_general(
        a, b, (over, ((), ())), precision=HIGHEST, preferred_element_type=jnp.float32
    )


def inverse_factor(gram):
    width = gram.shape[0]
    left, right = gram, eye(width)
    row_id = lax.broadcasted_iota(jnp.int32, (BLOCK, width), 0)
    done = []
    for start in range(0, width, BLOCK):
        p, e = left[:BLOCK], right[:BLOCK]
        pivots = jnp.zeros((BLOCK, width), jnp.float32)
        for base in range(0, BLOCK, TOGETHER):
            columns = [
                jnp.broadcast_to(p[:, start + s:start + s + 1], (BLOCK, width))
                for s in range(base, base + TOGETHER)
            ]
            for number in range(TOGETHER):
                s = base + number
                pivot = columns[number][s:s + 1]
                pivots = jnp.where(row_id == s, pivot, pivots)
                ratio = jnp.where(row_id > s, columns[number] * (1.0 / pivot), 0.0)
                for later in range(number + 1, TOGETHER):
                    columns[later] = columns[later] - ratio * columns[later][s:s + 1]
                p, e = p - ratio * p[s:s + 1], e - ratio * e[s:s + 1]
        scale = 1.0 / jnp.sqrt(pivots)
        p, e = p * scale, e * scale
        done.append(e)
        if start + BLOCK < width:
            change = outer(p, jnp.concatenate([p, e], axis=1))
            left = left[BLOCK:] - change[start + BLOCK:, :width]
            right = right[BLOCK:] - change[start + BLOCK:, width:]
    return jnp.concatenate(done, axis=0)


def eye(width):
    rows = lax.broadcasted_iota(jnp.int32, (width, width), 0)
    return jnp.where(rows == lax.broadcasted_iota(jnp.int32, (width, width), 1), 1.0, 0.0)


def coefficients(sums, inv0, corner, inv1, factor_scale, width, col):
    scaled_eye = factor_scale * eye(width)
    down, turned = ((0,), (0,)), ((1,), (1,))
    cross0 = product(inv0, sums[:width])
    seen = jnp.where(col == 0, factor_scale * product(sums, inv0, turned), sums)
    cross1 = product(jnp.concatenate([corner, inv1], axis=1), seen)
    t1 = jnp.where(col == 1, -scaled_eye, jnp.where(col == 0, 0.0, cross1))
    t0 = jnp.where(col == 0, -scaled_eye, jnp.where(col == 1, 0.0, cross0))
    x1 = product(inv1, t1, down)
    x0 = product(inv0, t0, down) + product(corner, t1, down)
    return cross0, cross1, jnp.concatenate([x0, x1], axis=0)


def halves(a):
    high = a.astype(jnp.bfloat16)
    return high, (a - high.astype(jnp.float32)).astype(jnp.bfloat16)


def pieces(start, stop, size):
    return [(at, min(size, stop - at)) for at in range(start, stop, size)]


def kernel(
    n_row, n_x, n_z, late, factor_scale,
    matrix_ref, r_ref, out_ref,
    panels, mine, mixed, total, parts, theirs,
    late_rows, late_sums, late_parts, late_total, late_in, full, factors,
    load_sem, recv_sem, send_sem, extra_send, extra_recv, gather_send, gather_recv,
    scatter_send, scatter_recv, back_send, back_recv, swap_sem,
    rows_send, rows_recv, part_send, part_recv, late_send, late_recv,
):
    rows, width = mine.shape
    steps = rows // TILE
    early = steps - late
    half = early // 2
    granule = GROUP * TILE
    row = lax.axis_index("row")
    col = lax.axis_index("col")
    x = lax.rem(col, n_x)
    z = col // n_x

    barrier = pltpu.get_barrier_semaphore()
    greeted = [
        (x > 0, col - 1), (x < n_x - 1, col + 1), (z > 0, col - n_x), (z < n_z - 1, col + n_x),
        (z > 1, x),
    ]
    greeted += [(z == 0, x + other * n_x) for other in range(2, n_z)]
    peers = n_row - 1
    for there, other in greeted:
        peers += jnp.where(there, 1, 0)

        @pl.when(there)
        def _():
            pl.semaphore_signal(barrier, inc=1, device_id={"col": other}, device_id_type=MESH)
    for step in range(1, n_row):
        peer = lax.rem(row + step, n_row)
        pl.semaphore_signal(barrier, inc=1, device_id={"row": peer}, device_id_type=MESH)
    load_mine = pltpu.make_async_copy(matrix_ref, mine, load_sem.at[0])
    load_mine.start()
    mixed[...] = jnp.zeros_like(mixed)
    pl.semaphore_wait(barrier, peers)

    def tile_at(index):
        return pl.ds(pl.multiple_of(index * TILE, TILE), TILE)

    def children(panel):
        return (
            (jnp.logical_and(x == panel, z < n_z - 1), col + n_x),
            (jnp.logical_and(x >= panel, x < n_x - 1), col + 1),
            (jnp.logical_and(x <= panel, x > 0), col - 1),
        )

    def forward(panel, index, source, which=(0, 1, 2)):
        for child, (there, other) in enumerate(children(panel)):
            if child not in which:
                continue

            @pl.when(there)
            def _():
                pltpu.make_async_remote_copy(
                    src_ref=source.at[tile_at(index)],
                    dst_ref=panels.at[panel, tile_at(index)],
                    send_sem=send_sem.at[panel, child],
                    recv_sem=recv_sem.at[panel, index],
                    device_id={"col": other},
                    device_id_type=MESH,
                ).start()

    def take(panel, index):
        here = panels.at[panel, tile_at(index)]
        pltpu.make_async_copy(here, here, recv_sem.at[panel, index]).wait()
        forward(panel, index, panels.at[panel])

    def place(panel, step):
        turned = jnp.where(panel == 1, early - 1 - (step - late), step - late)
        return jnp.where(step < late, early + step, turned)

    def both(at):
        return jnp.concatenate([panels[0, at], panels[1, at]], axis=1)

    def granule_at(index):
        return pl.ds(pl.multiple_of(index * granule, granule), granule)

    def cut(size, index):
        return pl.ds(pl.multiple_of(index * size, size), size)

    share = mixed.shape[0] // n_row
    third = width // n_row
    side = 3 * third // 2

    def row_copies(source, target, send, recv):
        copies = []
        for step in range(1, n_row):
            peer = lax.rem(row + step, n_row)
            copies.append(pltpu.make_async_remote_copy(
                src_ref=source(peer),
                dst_ref=target(step),
                send_sem=send.at[step - 1],
                recv_sem=recv.at[step - 1],
                device_id={"row": peer},
                device_id_type=MESH,
            ))
            copies[-1].start()
        return copies

    def scatter(source, size, turn):
        return row_copies(
            lambda peer: source(peer), lambda step: parts.at[turn, step - 1, pl.ds(0, size)],
            scatter_send.at[turn], scatter_recv.at[turn],
        )

    def settle(copies, source, size, turn, extra=None):
        summed = source(row)[...]
        if extra is not None:
            summed += extra()
        for step, copy in enumerate(copies):
            copy.wait_recv()
            summed += parts[turn, step, :size]
        here = total.at[turn, cut(size, row)]
        here[...] = summed
        return row_copies(
            lambda peer: here, lambda step: here, back_send.at[turn], back_recv.at[turn]
        )

    def mixed_part(peer):
        return mixed.at[cut(share, peer)]

    def extra_part(panel):
        return factors.at[row, pl.ds(pl.multiple_of(panel * side, side), side)]

    def forward_extra(panel):
        for child, (there, other) in enumerate(children(panel)):
            @pl.when(there)
            def _():
                pltpu.make_async_remote_copy(
                    src_ref=extra_part(panel),
                    dst_ref=extra_part(panel),
                    send_sem=extra_send.at[panel, child],
                    recv_sem=extra_recv.at[panel],
                    device_id={"col": other},
                    device_id_type=MESH,
                ).start()

    def take_extra(panel):
        here = extra_part(panel)
        pltpu.make_async_copy(here, here, extra_recv.at[panel]).wait()
        forward_extra(panel)

    def gather_factors():
        here = factors.at[row]
        return row_copies(lambda peer: here, lambda step: here, gather_send, gather_recv)

    def read_factors():
        return [
            jnp.concatenate(
                [factors[part, kind * third:(kind + 1) * third] for part in range(n_row)], axis=0
            )
            for kind in range(3)
        ]

    def solve(sums, inv0, corner, inv1):
        cross0, cross1, mix = coefficients(sums, inv0, corner, inv1, factor_scale, width, col)
        r_ref[0] = cross0 / factor_scale
        r_ref[1] = cross1 / factor_scale
        mix_high, mix_low = halves(mix)
        return mix_high, jnp.concatenate([mix_high, mix_low], axis=1)

    def update(mix, start, size):
        mix_high, mix_both = mix
        at = pl.ds(start, size)
        high, low = halves(both(at))
        main = jnp.dot(high, mix_both, preferred_element_type=jnp.float32)
        rest = jnp.dot(low, mix_high, preferred_element_type=jnp.float32)
        removed = main[:, :width] + (main[:, width:] + rest)
        out_ref[at] = jnp.where(col >= PANELS, mine[at], 0.0) - removed

    def sum_late(block):
        here = late_rows.at[block]
        pltpu.make_async_copy(here, here, rows_recv.at[block]).wait()
        late_sums[block] = jnp.zeros_like(late_sums[block])

        @pl.loop(0, late // GROUP)
        def _(index):
            at = pl.ds(pl.multiple_of(early * TILE + index * granule, granule), granule)
            late_sums[block] += outer(both(at), late_rows[block, granule_at(index)])

    def scatter_late():
        return row_copies(
            lambda peer: late_sums.at[:, cut(share, peer)], lambda step: late_parts.at[step - 1],
            part_send, part_recv,
        )

    def late_copies():
        return [
            pltpu.make_async_remote_copy(
                src_ref=late_total.at[block],
                dst_ref=late_in,
                send_sem=late_send.at[block],
                recv_sem=late_recv,
                device_id={"col": x + (block + 1) * n_x},
                device_id_type=MESH,
            )
            for block in range(n_z - 1)
        ]

    def send_late(copies):
        summed = late_sums[:, cut(share, row)]
        for step, copy in enumerate(copies):
            copy.wait_recv()
            summed += late_parts[step]
        late_total[...] = summed
        sends = late_copies()
        for copy in sends:
            copy.start()
        return sends

    def finish_sends(copies):
        for copy in copies:
            copy.wait_send()

    def finish(copies):
        for copy in copies:
            copy.wait_recv()

    @pl.when(col < PANELS)
    def _():
        second = 1 - col
        first = col == 0
        blocks = list(range(n_z - 1))

        @pl.loop(0, early)
        def _(index):
            forward(col, index, matrix_ref, (0,))

        @pl.loop(0, late)
        def _(step):
            forward(col, place(col, step), matrix_ref, (1, 2))

        load_mine.wait()
        own = pltpu.make_async_copy(mine, panels.at[col], load_sem.at[1])
        own.start()
        block = pl.ds(pl.multiple_of(col * width, width), width)
        other_block = pl.ds(pl.multiple_of(second * width, width), width)

        def block_part(panel):
            def part(peer):
                start = panel * width + peer * third
                return mixed.at[pl.ds(pl.multiple_of(start, third), third)]
            return part

        def swap(turn):
            copy = pltpu.make_async_remote_copy(
                src_ref=total.at[turn, pl.ds(0, width)],
                dst_ref=theirs.at[turn],
                send_sem=swap_sem.at[turn, 0],
                recv_sem=swap_sem.at[turn, 1],
                device_id={"col": 1 - col},
                device_id_type=MESH,
            )
            copy.start()
            return copy

        @pl.loop(0, rows // granule)
        def _(index):
            at = granule_at(index)
            mixed[block] += outer(mine[at], mine[at])

        copies = scatter(block_part(col), third, 0)
        backs = settle(copies, block_part(col), third, 0)
        finish(backs)
        sent = copies + backs
        grams = swap(0)

        @pl.loop(late, late + half + AHEAD)
        def _(step):
            forward(col, place(col, step), matrix_ref, (1, 2))

        grams.wait()
        gram0 = jnp.where(first, total[0, :width], theirs[0])
        full[0] = inverse_factor(gram0)
        own.wait()

        @pl.loop(0, late)
        def _(step):
            take(second, place(second, step))

        @pl.when(first)
        def _():
            @pl.loop(early // GROUP, steps // GROUP)
            def _(index):
                at = granule_at(index)
                mixed[other_block] += outer(panels[second, at], mine[at])

        def meet(start, stop):
            @pl.loop(start, stop)
            def _(group):
                for step in range(GROUP):
                    take(second, place(second, late + group * GROUP + step))
                at = granule_at(place(second, late + group * GROUP) // GROUP)
                mixed[other_block] += outer(panels[second, at], mine[at])

        for number in blocks[:1:-1]:
            sum_late(number)
        meet(0, half // GROUP // 2)
        for number in blocks[1:2]:
            sum_late(number)
        meet(half // GROUP // 2, half // GROUP)
        copies = scatter(block_part(second), third, 1)
        sum_late(0)
        late_scatter = scatter_late()
        backs = settle(copies, block_part(second), third, 1)
        finish(backs)
        sent += copies + backs
        crossed = swap(1)

        @pl.loop(late + half + AHEAD, steps)
        def _(step):
            forward(col, place(col, step), matrix_ref, (1, 2))

        late_sends = send_late(late_scatter)
        crossed.wait()
        inv0 = full[0]
        gram0 = jnp.where(first, total[0, :width], theirs[0])
        gram1 = jnp.where(first, theirs[0], total[0, :width])
        ours, other = total[1, :width], theirs[1]
        gram01 = jnp.where(first, ours.T + other, ours + other.T)
        r01 = product(inv0, gram01)
        inv1 = inverse_factor(gram1 - product(r01, r01, ((0,), (0,))))
        corner = -product(product(inv1, r01, ((1,), (1,))), inv0)
        full[1], full[2] = corner, inv1
        whole = jnp.concatenate([full[kind, cut(third, row)] for kind in range(3)], axis=0)
        extra_part(col)[...] = jnp.where(first, whole[:side], whole[side:])
        forward_extra(col)

        @pl.loop(early, steps)
        def _(index):
            forward(col, index, matrix_ref, (0,))

        take_extra(second)
        sums = jnp.concatenate(
            [jnp.where(first, gram0, gram01), jnp.where(first, gram01.T, gram1)], axis=0
        )
        mix = solve(sums, inv0, corner, inv1)

        @pl.loop(late + half, steps)
        def _(step):
            take(second, place(second, step))

        @pl.loop(0, rows // CHUNK)
        def _(index):
            update(mix, pl.multiple_of(index * CHUNK, CHUNK), CHUNK)

        finish_sends(late_scatter + late_sends + sent)

    @pl.when(z > 0)
    def _():
        main = jnp.where(x == 1, 1, 0)
        second = 1 - main
        last = pl.ds(early * TILE, late * TILE)
        for block in range(n_z - 1):
            @pl.when(z == block + 1)
            def _():
                pltpu.make_async_remote_copy(
                    src_ref=matrix_ref.at[last],
                    dst_ref=late_rows.at[block],
                    send_sem=rows_send,
                    recv_sem=rows_recv.at[block],
                    device_id={"col": x},
                    device_id_type=MESH,
                ).start()
        load_mine.wait()

        def add(index):
            at = granule_at(index)
            mixed[...] += outer(both(at), mine[at])

        def slot(index):
            take(main, index)
            take(second, index - LAG)

        behind = LAG // GROUP

        @pl.loop(0, LAG)
        def _(index):
            take(main, index)

        @pl.loop(behind, early // GROUP)
        def _(group):
            for step in range(GROUP):
                slot(group * GROUP + step)
            add(group - behind)

        spot = [early]

        def slots(count):
            stop = min(spot[0] + count, steps)

            @pl.loop(spot[0], stop)
            def _(index):
                slot(index)
            spot[0] = stop

        take_extra(main)
        slots(LAG)
        take_extra(second)
        gathers = gather_factors()

        @pl.loop(early // GROUP - behind, early // GROUP)
        def _(group):
            add(group)

        copies = scatter(mixed_part, share, 0)
        slots(3)

        def brought():
            pltpu.make_async_copy(late_in, late_in, late_recv).wait()
            return late_in[...]

        backs = settle(copies, mixed_part, share, 0, brought)
        slots(3)
        finish(gathers)
        inverses = read_factors()
        finish(backs)
        mix = solve(total[0], *inverses)
        work = pieces(0, early * TILE, CHUNK)
        left_over = steps - spot[0]
        for number, (start, size) in enumerate(work):
            update(mix, start, size)
            slots(left_over * (number + 1) // (2 * len(work)) - (spot[0] - steps + left_over))
        reach = early * TILE
        for start, size in pieces(reach, rows, 2 * granule):
            need = (start + size) // TILE
            if need == steps:
                break
            slots(max(0, min(need + LAG, steps) - spot[0]))
            update(mix, start, size)
            reach = start + size
        slots(steps - spot[0])

        @pl.loop(steps - LAG, steps)
        def _(index):
            take(second, index)

        update(mix, reach, rows - reach)
        finish_sends(copies + backs + gathers)
        pltpu.make_async_remote_copy(
            src_ref=matrix_ref.at[last],
            dst_ref=late_rows.at[0],
            send_sem=rows_send,
            recv_sem=rows_recv.at[0],
            device_id={"col": x},
            device_id_type=MESH,
        ).wait_send()

    if n_x > PANELS:
        @pl.when(jnp.logical_and(z == 0, col >= PANELS))
        def _():
            load_mine.wait()

            @pl.loop(0, late)
            def _(step):
                take(0, place(0, step))
                take(1, place(1, step))

            for block in range(n_z - 1):
                sum_late(block)
            late_scatter = scatter_late()
            late_sends = send_late(late_scatter)

            @pl.loop(late, steps)
            def _(step):
                take(0, place(0, step))
                take(1, place(1, step))

            @pl.loop(0, rows // granule)
            def _(index):
                at = granule_at(index)
                mixed[...] += outer(both(at), mine[at])

            take_extra(0)
            take_extra(1)
            gathers = gather_factors()
            copies = scatter(mixed_part, share, 0)
            backs = settle(copies, mixed_part, share, 0)
            finish(gathers)
            inverses = read_factors()
            finish(backs)
            mix = solve(total[0], *inverses)

            @pl.loop(0, rows // CHUNK)
            def _(index):
                update(mix, pl.multiple_of(index * CHUNK, CHUNK), CHUNK)

            finish_sends(late_scatter + late_sends + copies + backs + gathers)

    for panel in range(PANELS):
        for child, (there, other) in enumerate(children(panel)):
            @pl.when(there)
            def _():
                pltpu.make_async_remote_copy(
                    src_ref=panels.at[panel],
                    dst_ref=panels.at[panel],
                    send_sem=send_sem.at[panel, child],
                    recv_sem=recv_sem.at[panel, 0],
                    device_id={"col": other},
                    device_id_type=MESH,
                ).wait_send()
                pltpu.make_async_remote_copy(
                    src_ref=extra_part(panel),
                    dst_ref=extra_part(panel),
                    send_sem=extra_send.at[panel, child],
                    recv_sem=extra_recv.at[panel],
                    device_id={"col": other},
                    device_id_type=MESH,
                ).wait_send()


def solution(mesh):
    n_row, n_col = mesh.shape["row"], mesh.shape["col"]
    n_x = max(PANELS, n_row // 2)
    n_z = n_col // n_x
    assert n_x * n_z == n_col and n_z > 1

    def local(matrix):
        rows, width = matrix.shape
        steps = rows // TILE
        late = LATE
        assert rows % CHUNK == 0 and late % GROUP == 0 and (steps - late) % (2 * GROUP) == 0
        deep = PANELS * width
        share, third = deep // n_row, width // n_row
        vmem = pltpu.VMEM
        f32 = jnp.float32
        dma = pltpu.SemaphoreType.DMA
        in_vmem = pl.BlockSpec(memory_space=vmem)
        return pl.pallas_call(
            functools.partial(kernel, n_row, n_x, n_z, late, math.sqrt(rows * n_row)),
            out_shape=(
                jax.ShapeDtypeStruct((PANELS, width, width), f32),
                jax.ShapeDtypeStruct((rows, width), f32),
            ),
            in_specs=[pl.BlockSpec(memory_space=pl.ANY)],
            out_specs=(in_vmem, in_vmem),
            scratch_shapes=[
                vmem((PANELS, rows, width), f32),
                vmem((rows, width), f32),
                vmem((deep, width), f32),
                vmem((2, deep, width), f32),
                vmem((2, n_row - 1, share, width), f32),
                vmem((2, width, width), f32),
                vmem((n_z - 1, late * TILE, width), f32),
                vmem((n_z - 1, deep, width), f32),
                vmem((n_row - 1, n_z - 1, share, width), f32),
                vmem((n_z - 1, share, width), f32),
                vmem((share, width), f32),
                vmem((3, width, width), f32),
                vmem((n_row, 3 * third, width), f32),
                dma((2,)),
                dma((PANELS, steps)),
                dma((PANELS, 3)),
                dma((PANELS, 3)),
                dma((PANELS,)),
                dma((n_row - 1,)),
                dma((n_row - 1,)),
                dma((2, n_row - 1)),
                dma((2, n_row - 1)),
                dma((2, n_row - 1)),
                dma((2, n_row - 1)),
                dma((2, 2)),
                dma,
                dma((n_z - 1,)),
                dma((n_row - 1,)),
                dma((n_row - 1,)),
                dma((n_z - 1,)),
                dma,
            ],
            compiler_params=pltpu.CompilerParams(
                collective_id=0, has_side_effects=True, vmem_limit_bytes=47 * 1024 * 1024
            ),
        )(matrix)

    return jax.shard_map(
        local,
        mesh=mesh,
        in_specs=(P("row", "col"),),
        out_specs=(P(None, None, "col"), P("row", "col")),
        check_vma=False,
    )
```

```python
import functools
import math

import jax
import jax.numpy as jnp
from jax import lax
from jax.experimental import pallas as pl
from jax.experimental.pallas import tpu as pltpu
from jax.sharding import PartitionSpec as P

MESH = pl.DeviceIdType.MESH
HIGHEST = lax.Precision.HIGHEST
PANELS = 2
BLOCK = 32
TOGETHER = 16
TILE = 64
GROUP = 4
LAG = 8
LATE = 24
FIRST = 36
AHEAD = 12
HOLD = 10
BATCH = 8
DEEP = 512
CHUNK = 1024


def outer(a, b):
    return lax.dot_general(
        a, b, (((0,), (0,)), ((), ())), precision=HIGHEST, preferred_element_type=jnp.float32
    )


def product(a, b, over=((1,), (0,))):
    return lax.dot_general(
        a, b, (over, ((), ())), precision=HIGHEST, preferred_element_type=jnp.float32
    )


def inverse_factor(gram):
    width = gram.shape[0]
    left, right = gram, eye(width)
    row_id = lax.broadcasted_iota(jnp.int32, (BLOCK, width), 0)
    done = []
    for start in range(0, width, BLOCK):
        p, e = left[:BLOCK], right[:BLOCK]
        pivots = jnp.zeros((BLOCK, width), jnp.float32)
        for base in range(0, BLOCK, TOGETHER):
            columns = [
                jnp.broadcast_to(p[:, start + s:start + s + 1], (BLOCK, width))
                for s in range(base, base + TOGETHER)
            ]
            for number in range(TOGETHER):
                s = base + number
                pivot = columns[number][s:s + 1]
                pivots = jnp.where(row_id == s, pivot, pivots)
                ratio = jnp.where(row_id > s, columns[number] * (1.0 / pivot), 0.0)
                for later in range(number + 1, TOGETHER):
                    columns[later] = columns[later] - ratio * columns[later][s:s + 1]
                p, e = p - ratio * p[s:s + 1], e - ratio * e[s:s + 1]
        scale = 1.0 / jnp.sqrt(pivots)
        p, e = p * scale, e * scale
        done.append(e)
        if start + BLOCK < width:
            change = outer(p, jnp.concatenate([p, e], axis=1))
            left = left[BLOCK:] - change[start + BLOCK:, :width]
            right = right[BLOCK:] - change[start + BLOCK:, width:]
    return jnp.concatenate(done, axis=0)


def eye(width):
    rows = lax.broadcasted_iota(jnp.int32, (width, width), 0)
    return jnp.where(rows == lax.broadcasted_iota(jnp.int32, (width, width), 1), 1.0, 0.0)


def coefficients(sums, inv0, corner, inv1, factor_scale, width, col):
    scaled_eye = factor_scale * eye(width)
    down, turned = ((0,), (0,)), ((1,), (1,))
    cross0 = product(inv0, sums[:width])
    seen = jnp.where(col == 0, factor_scale * product(sums, inv0, turned), sums)
    cross1 = product(jnp.concatenate([corner, inv1], axis=1), seen)
    t1 = jnp.where(col == 1, -scaled_eye, jnp.where(col == 0, 0.0, cross1))
    t0 = jnp.where(col == 0, -scaled_eye, jnp.where(col == 1, 0.0, cross0))
    x1 = product(inv1, t1, down)
    x0 = product(inv0, t0, down) + product(corner, t1, down)
    return cross0, cross1, jnp.concatenate([x0, x1], axis=0)


def halves(a):
    high = a.astype(jnp.bfloat16)
    return high, (a - high.astype(jnp.float32)).astype(jnp.bfloat16)


def pieces(start, stop, size):
    return [(at, min(size, stop - at)) for at in range(start, stop, size)]


def kernel(
    n_row, n_x, n_z, late, factor_scale,
    matrix_ref, r_ref, out_ref,
    panels, mine, mixed, total, parts, theirs,
    late_rows, late_sums, late_parts, late_total, late_in, full, factors,
    load_sem, recv_sem, send_sem, extra_send, extra_recv, gather_send, gather_recv,
    scatter_send, scatter_recv, back_send, back_recv, swap_sem,
    rows_send, rows_recv, part_send, part_recv, late_send, late_recv,
):
    rows, width = mine.shape
    steps = rows // TILE
    early = steps - late
    half = steps // 2
    granule = GROUP * TILE
    row = lax.axis_index("row")
    col = lax.axis_index("col")
    x = lax.rem(col, n_x)
    z = col // n_x

    barrier = pltpu.get_barrier_semaphore()
    greeted = [
        (x > 0, col - 1), (x < n_x - 1, col + 1), (z > 0, col - n_x), (z < n_z - 1, col + n_x),
        (z > 1, x),
    ]
    greeted += [(z == 0, x + other * n_x) for other in range(2, n_z)]
    peers = n_row - 1
    for there, other in greeted:
        peers += jnp.where(there, 1, 0)

        @pl.when(there)
        def _():
            pl.semaphore_signal(barrier, inc=1, device_id={"col": other}, device_id_type=MESH)
    for step in range(1, n_row):
        peer = lax.rem(row + step, n_row)
        pl.semaphore_signal(barrier, inc=1, device_id={"row": peer}, device_id_type=MESH)
    load_mine = pltpu.make_async_copy(matrix_ref, mine, load_sem.at[0])
    load_mine.start()
    mixed[...] = jnp.zeros_like(mixed)
    pl.semaphore_wait(barrier, peers)

    def tile_at(index):
        return pl.ds(pl.multiple_of(index * TILE, TILE), TILE)

    def children(panel):
        return (
            (jnp.logical_and(x == panel, z < n_z - 1), col + n_x),
            (jnp.logical_and(x >= panel, x < n_x - 1), col + 1),
            (jnp.logical_and(x <= panel, x > 0), col - 1),
        )

    def forward(panel, index, source, which=(0, 1, 2)):
        for child, (there, other) in enumerate(children(panel)):
            if child not in which:
                continue

            @pl.when(there)
            def _():
                pltpu.make_async_remote_copy(
                    src_ref=source.at[tile_at(index)],
                    dst_ref=panels.at[panel, tile_at(index)],
                    send_sem=send_sem.at[panel, child],
                    recv_sem=recv_sem.at[panel, index],
                    device_id={"col": other},
                    device_id_type=MESH,
                ).start()

    def take(panel, index):
        here = panels.at[panel, tile_at(index)]
        pltpu.make_async_copy(here, here, recv_sem.at[panel, index]).wait()
        forward(panel, index, panels.at[panel])

    def place(panel, step):
        up = jnp.where(step < half + late, early - half, -late)
        down = jnp.where(step < late, early, jnp.where(step < half, half - late, -half))
        return step + jnp.where(panel == 1, down, jnp.where(step < half, 0, up))

    def both(at):
        return jnp.concatenate([panels[0, at], panels[1, at]], axis=1)

    def granule_at(index):
        return pl.ds(pl.multiple_of(index * granule, granule), granule)

    def cut(size, index):
        return pl.ds(pl.multiple_of(index * size, size), size)

    share = mixed.shape[0] // n_row
    third = width // n_row
    side = 3 * third // 2

    def row_copies(source, target, send, recv):
        copies = []
        for step in range(1, n_row):
            peer = lax.rem(row + step, n_row)
            copies.append(pltpu.make_async_remote_copy(
                src_ref=source(peer),
                dst_ref=target(step),
                send_sem=send.at[step - 1],
                recv_sem=recv.at[step - 1],
                device_id={"row": peer},
                device_id_type=MESH,
            ))
            copies[-1].start()
        return copies

    def scatter(source, size, turn):
        return row_copies(
            lambda peer: source(peer), lambda step: parts.at[turn, step - 1, pl.ds(0, size)],
            scatter_send.at[turn], scatter_recv.at[turn],
        )

    def settle(copies, source, size, turn, extra=None):
        summed = source(row)[...]
        if extra is not None:
            summed += extra()
        for step, copy in enumerate(copies):
            copy.wait_recv()
            summed += parts[turn, step, :size]
        here = total.at[turn, cut(size, row)]
        here[...] = summed
        return row_copies(
            lambda peer: here, lambda step: here, back_send.at[turn], back_recv.at[turn]
        )

    def mixed_part(peer):
        return mixed.at[cut(share, peer)]

    def extra_part(panel):
        return factors.at[row, pl.ds(pl.multiple_of(panel * side, side), side)]

    def forward_extra(panel):
        for child, (there, other) in enumerate(children(panel)):
            @pl.when(there)
            def _():
                pltpu.make_async_remote_copy(
                    src_ref=extra_part(panel),
                    dst_ref=extra_part(panel),
                    send_sem=extra_send.at[panel, child],
                    recv_sem=extra_recv.at[panel],
                    device_id={"col": other},
                    device_id_type=MESH,
                ).start()

    def take_extra(panel):
        here = extra_part(panel)
        pltpu.make_async_copy(here, here, extra_recv.at[panel]).wait()
        forward_extra(panel)

    def gather_factors():
        here = factors.at[row]
        return row_copies(lambda peer: here, lambda step: here, gather_send, gather_recv)

    def read_factors():
        return [
            jnp.concatenate(
                [factors[part, kind * third:(kind + 1) * third] for part in range(n_row)], axis=0
            )
            for kind in range(3)
        ]

    def solve(sums, inv0, corner, inv1):
        cross0, cross1, mix = coefficients(sums, inv0, corner, inv1, factor_scale, width, col)
        r_ref[0] = cross0 / factor_scale
        r_ref[1] = cross1 / factor_scale
        mix_high, mix_low = halves(mix)
        return mix_high, jnp.concatenate([mix_high, mix_low], axis=1)

    def update(mix, start, size):
        mix_high, mix_both = mix
        at = pl.ds(start, size)
        high, low = halves(both(at))
        main = jnp.dot(high, mix_both, preferred_element_type=jnp.float32)
        rest = jnp.dot(low, mix_high, preferred_element_type=jnp.float32)
        removed = main[:, :width] + (main[:, width:] + rest)
        out_ref[at] = jnp.where(col >= PANELS, mine[at], 0.0) - removed

    def sum_late(block):
        here = late_rows.at[block]
        pltpu.make_async_copy(here, here, rows_recv.at[block]).wait()
        late_sums[block] = jnp.zeros_like(late_sums[block])

        @pl.loop(0, late * TILE // DEEP)
        def _(index):
            at = pl.ds(pl.multiple_of(early * TILE + index * DEEP, DEEP), DEEP)
            late_sums[block] += outer(both(at), late_rows[block, cut(DEEP, index)])

    def scatter_late():
        return row_copies(
            lambda peer: late_sums.at[:, cut(share, peer)], lambda step: late_parts.at[step - 1],
            part_send, part_recv,
        )

    def late_copies():
        return [
            pltpu.make_async_remote_copy(
                src_ref=late_total.at[block],
                dst_ref=late_in,
                send_sem=late_send.at[block],
                recv_sem=late_recv,
                device_id={"col": x + (block + 1) * n_x},
                device_id_type=MESH,
            )
            for block in range(n_z - 1)
        ]

    def send_late(copies):
        summed = late_sums[:, cut(share, row)]
        for step, copy in enumerate(copies):
            copy.wait_recv()
            summed += late_parts[step]
        late_total[...] = summed
        sends = late_copies()
        for copy in sends:
            copy.start()
        return sends

    def finish_sends(copies):
        for copy in copies:
            copy.wait_send()

    def finish(copies):
        for copy in copies:
            copy.wait_recv()

    @pl.when(col < PANELS)
    def _():
        second = 1 - col
        first = col == 0

        @pl.loop(0, early)
        def _(index):
            forward(col, index, matrix_ref, (0,))

        @pl.loop(0, FIRST)
        def _(step):
            forward(col, place(col, step), matrix_ref, (1, 2))

        load_mine.wait()
        own = pltpu.make_async_copy(mine, panels.at[col], load_sem.at[1])
        own.start()
        block = pl.ds(pl.multiple_of(col * width, width), width)
        other_block = pl.ds(pl.multiple_of(second * width, width), width)

        def block_part(panel):
            def part(peer):
                start = panel * width + peer * third
                return mixed.at[pl.ds(pl.multiple_of(start, third), third)]
            return part

        def swap(turn):
            copy = pltpu.make_async_remote_copy(
                src_ref=total.at[turn, pl.ds(0, width)],
                dst_ref=theirs.at[turn],
                send_sem=swap_sem.at[turn, 0],
                recv_sem=swap_sem.at[turn, 1],
                device_id={"col": 1 - col},
                device_id_type=MESH,
            )
            copy.start()
            return copy

        @pl.loop(0, rows // granule)
        def _(index):
            at = granule_at(index)
            mixed[block] += outer(mine[at], mine[at])

        copies = scatter(block_part(col), third, 0)
        backs = settle(copies, block_part(col), third, 0)
        finish(backs)
        sent = copies + backs
        grams = swap(0)

        @pl.loop(FIRST, half + AHEAD)
        def _(step):
            forward(col, place(col, step), matrix_ref, (1, 2))

        grams.wait()
        gram0 = jnp.where(first, total[0, :width], theirs[0])
        full[0] = inverse_factor(gram0)
        own.wait()

        @pl.loop(0, half // GROUP)
        def _(group):
            for step in range(GROUP):
                take(second, place(second, group * GROUP + step))
            at = granule_at(place(second, group * GROUP) // GROUP)
            mixed[other_block] += outer(panels[second, at], mine[at])

        copies = scatter(block_part(second), third, 1)
        backs = settle(copies, block_part(second), third, 1)
        finish(backs)
        sent += copies + backs
        crossed = swap(1)

        @pl.loop(half + AHEAD, steps)
        def _(step):
            forward(col, place(col, step), matrix_ref, (1, 2))

        crossed.wait()
        inv0 = full[0]
        gram0 = jnp.where(first, total[0, :width], theirs[0])
        gram1 = jnp.where(first, theirs[0], total[0, :width])
        ours, other = total[1, :width], theirs[1]
        gram01 = jnp.where(first, ours.T + other, ours + other.T)
        r01 = product(inv0, gram01)
        inv1 = inverse_factor(gram1 - product(r01, r01, ((0,), (0,))))
        corner = -product(product(inv1, r01, ((1,), (1,))), inv0)
        full[1], full[2] = corner, inv1
        whole = jnp.concatenate([full[kind, cut(third, row)] for kind in range(3)], axis=0)
        extra_part(col)[...] = jnp.where(first, whole[:side], whole[side:])
        forward_extra(col)

        @pl.loop(early, early + HOLD)
        def _(index):
            forward(col, index, matrix_ref, (0,))

        @pl.loop(half, half + late)
        def _(step):
            take(second, place(second, step))

        for number in reversed(range(n_z - 1)):
            sum_late(number)
        late_scatter = scatter_late()
        late_sends = send_late(late_scatter)

        @pl.loop(early + HOLD, steps)
        def _(index):
            forward(col, index, matrix_ref, (0,))

        sums = jnp.concatenate(
            [jnp.where(first, gram0, gram01), jnp.where(first, gram01.T, gram1)], axis=0
        )
        mix = solve(sums, inv0, corner, inv1)

        def renew(group):
            start = place(second, group * BATCH) * TILE
            update(mix, pl.multiple_of(start, BATCH * TILE), BATCH * TILE)

        @pl.loop(0, (half + late) // BATCH)
        def _(group):
            renew(group)

        @pl.loop((half + late) // BATCH, steps // BATCH)
        def _(group):
            for step in range(BATCH):
                take(second, place(second, group * BATCH + step))
            renew(group)

        take_extra(second)
        finish_sends(late_scatter + late_sends + sent)

    @pl.when(z > 0)
    def _():
        main = jnp.where(x == 1, 1, 0)
        second = 1 - main
        last = pl.ds(early * TILE, late * TILE)
        for block in range(n_z - 1):
            @pl.when(z == block + 1)
            def _():
                pltpu.make_async_remote_copy(
                    src_ref=matrix_ref.at[last],
                    dst_ref=late_rows.at[block],
                    send_sem=rows_send,
                    recv_sem=rows_recv.at[block],
                    device_id={"col": x},
                    device_id_type=MESH,
                ).start()
        load_mine.wait()

        def add(index):
            at = granule_at(index)
            mixed[...] += outer(both(at), mine[at])

        def slot(index):
            take(main, index)
            take(second, index - LAG)

        behind = LAG // GROUP

        @pl.loop(0, LAG)
        def _(index):
            take(main, index)

        @pl.loop(behind, early // GROUP)
        def _(group):
            for step in range(GROUP):
                slot(group * GROUP + step)
            add(group - behind)

        spot = [early]

        def slots(count):
            stop = min(spot[0] + count, steps)

            @pl.loop(spot[0], stop)
            def _(index):
                slot(index)
            spot[0] = stop

        take_extra(main)
        slots(LAG)
        take_extra(second)
        gathers = gather_factors()

        @pl.loop(early // GROUP - behind, early // GROUP)
        def _(group):
            add(group)

        copies = scatter(mixed_part, share, 0)
        slots(6)

        def brought():
            pltpu.make_async_copy(late_in, late_in, late_recv).wait()
            return late_in[...]

        backs = settle(copies, mixed_part, share, 0, brought)
        slots(6)
        finish(gathers)
        inverses = read_factors()
        finish(backs)
        mix = solve(total[0], *inverses)
        work = pieces(0, early * TILE, CHUNK)
        left_over = steps - spot[0]
        for number, (start, size) in enumerate(work):
            update(mix, start, size)
            slots(left_over * (number + 1) // (2 * len(work)) - (spot[0] - steps + left_over))
        reach = early * TILE
        for start, size in pieces(reach, rows, 2 * granule):
            need = (start + size) // TILE
            if need == steps:
                break
            slots(max(0, min(need + LAG, steps) - spot[0]))
            update(mix, start, size)
            reach = start + size
        slots(steps - spot[0])

        @pl.loop(steps - LAG, steps)
        def _(index):
            take(second, index)

        update(mix, reach, rows - reach)
        finish_sends(copies + backs + gathers)
        pltpu.make_async_remote_copy(
            src_ref=matrix_ref.at[last],
            dst_ref=late_rows.at[0],
            send_sem=rows_send,
            recv_sem=rows_recv.at[0],
            device_id={"col": x},
            device_id_type=MESH,
        ).wait_send()

    if n_x > PANELS:
        @pl.when(jnp.logical_and(z == 0, col >= PANELS))
        def _():
            load_mine.wait()

            @pl.loop(0, steps)
            def _(step):
                take(0, place(0, step))
                take(1, place(1, step))

            for block in range(n_z - 1):
                sum_late(block)
            late_scatter = scatter_late()
            late_sends = send_late(late_scatter)

            @pl.loop(0, rows // granule)
            def _(index):
                at = granule_at(index)
                mixed[...] += outer(both(at), mine[at])

            take_extra(0)
            take_extra(1)
            gathers = gather_factors()
            copies = scatter(mixed_part, share, 0)
            backs = settle(copies, mixed_part, share, 0)
            finish(gathers)
            inverses = read_factors()
            finish(backs)
            mix = solve(total[0], *inverses)

            @pl.loop(0, rows // CHUNK)
            def _(index):
                update(mix, pl.multiple_of(index * CHUNK, CHUNK), CHUNK)

            finish_sends(late_scatter + late_sends + copies + backs + gathers)

    for panel in range(PANELS):
        for child, (there, other) in enumerate(children(panel)):
            @pl.when(there)
            def _():
                pltpu.make_async_remote_copy(
                    src_ref=panels.at[panel],
                    dst_ref=panels.at[panel],
                    send_sem=send_sem.at[panel, child],
                    recv_sem=recv_sem.at[panel, 0],
                    device_id={"col": other},
                    device_id_type=MESH,
                ).wait_send()
                pltpu.make_async_remote_copy(
                    src_ref=extra_part(panel),
                    dst_ref=extra_part(panel),
                    send_sem=extra_send.at[panel, child],
                    recv_sem=extra_recv.at[panel],
                    device_id={"col": other},
                    device_id_type=MESH,
                ).wait_send()


def solution(mesh):
    n_row, n_col = mesh.shape["row"], mesh.shape["col"]
    n_x = max(PANELS, n_row // 2)
    n_z = n_col // n_x
    assert n_x * n_z == n_col and n_z > 1

    def local(matrix):
        rows, width = matrix.shape
        steps = rows // TILE
        late = LATE
        assert rows % CHUNK == 0 and late * TILE % DEEP == 0
        assert late % BATCH == 0 and steps % (2 * BATCH) == 0 and late < steps // 2
        deep = PANELS * width
        share, third = deep // n_row, width // n_row
        vmem = pltpu.VMEM
        f32 = jnp.float32
        dma = pltpu.SemaphoreType.DMA
        in_vmem = pl.BlockSpec(memory_space=vmem)
        return pl.pallas_call(
            functools.partial(kernel, n_row, n_x, n_z, late, math.sqrt(rows * n_row)),
            out_shape=(
                jax.ShapeDtypeStruct((PANELS, width, width), f32),
                jax.ShapeDtypeStruct((rows, width), f32),
            ),
            in_specs=[pl.BlockSpec(memory_space=pl.ANY)],
            out_specs=(in_vmem, in_vmem),
            scratch_shapes=[
                vmem((PANELS, rows, width), f32),
                vmem((rows, width), f32),
                vmem((deep, width), f32),
                vmem((2, deep, width), f32),
                vmem((2, n_row - 1, share, width), f32),
                vmem((2, width, width), f32),
                vmem((n_z - 1, late * TILE, width), f32),
                vmem((n_z - 1, deep, width), f32),
                vmem((n_row - 1, n_z - 1, share, width), f32),
                vmem((n_z - 1, share, width), f32),
                vmem((share, width), f32),
                vmem((3, width, width), f32),
                vmem((n_row, 3 * third, width), f32),
                dma((2,)),
                dma((PANELS, steps)),
                dma((PANELS, 3)),
                dma((PANELS, 3)),
                dma((PANELS,)),
                dma((n_row - 1,)),
                dma((n_row - 1,)),
                dma((2, n_row - 1)),
                dma((2, n_row - 1)),
                dma((2, n_row - 1)),
                dma((2, n_row - 1)),
                dma((2, 2)),
                dma,
                dma((n_z - 1,)),
                dma((n_row - 1,)),
                dma((n_row - 1,)),
                dma((n_z - 1,)),
                dma,
            ],
            compiler_params=pltpu.CompilerParams(
                collective_id=0, has_side_effects=True, vmem_limit_bytes=47 * 1024 * 1024
            ),
        )(matrix)

    return jax.shard_map(
        local,
        mesh=mesh,
        in_specs=(P("row", "col"),),
        out_specs=(P(None, None, "col"), P("row", "col")),
        check_vma=False,
    )
```

```python
import functools
import math

import jax
import jax.numpy as jnp
from jax import lax
from jax.experimental import pallas as pl
from jax.experimental.pallas import tpu as pltpu
from jax.sharding import PartitionSpec as P

MESH = pl.DeviceIdType.MESH
HIGHEST = lax.Precision.HIGHEST
PANELS = 2
BLOCK = 32
TOGETHER = 16
TILE = 64
GROUP = 4
LAG = 8
LATE = 24
FIRST = 36
AHEAD = 12
HOLD = 8
BATCH = 8
DEEP = 512
CHUNK = 1024


def outer(a, b):
    return lax.dot_general(
        a, b, (((0,), (0,)), ((), ())), precision=HIGHEST, preferred_element_type=jnp.float32
    )


def product(a, b, over=((1,), (0,))):
    return lax.dot_general(
        a, b, (over, ((), ())), precision=HIGHEST, preferred_element_type=jnp.float32
    )


def inverse_factor(gram):
    width = gram.shape[0]
    left, right = gram, eye(width)
    row_id = lax.broadcasted_iota(jnp.int32, (BLOCK, width), 0)
    done = []
    for start in range(0, width, BLOCK):
        p, e = left[:BLOCK], right[:BLOCK]
        pivots = jnp.zeros((BLOCK, width), jnp.float32)
        for base in range(0, BLOCK, TOGETHER):
            columns = [
                jnp.broadcast_to(p[:, start + s:start + s + 1], (BLOCK, width))
                for s in range(base, base + TOGETHER)
            ]
            for number in range(TOGETHER):
                s = base + number
                pivot = columns[number][s:s + 1]
                pivots = jnp.where(row_id == s, pivot, pivots)
                ratio = jnp.where(row_id > s, columns[number] * (1.0 / pivot), 0.0)
                for later in range(number + 1, TOGETHER):
                    columns[later] = columns[later] - ratio * columns[later][s:s + 1]
                p, e = p - ratio * p[s:s + 1], e - ratio * e[s:s + 1]
        scale = 1.0 / jnp.sqrt(pivots)
        p, e = p * scale, e * scale
        done.append(e)
        if start + BLOCK < width:
            change = outer(p, jnp.concatenate([p, e], axis=1))
            left = left[BLOCK:] - change[start + BLOCK:, :width]
            right = right[BLOCK:] - change[start + BLOCK:, width:]
    return jnp.concatenate(done, axis=0)


def eye(width):
    rows = lax.broadcasted_iota(jnp.int32, (width, width), 0)
    return jnp.where(rows == lax.broadcasted_iota(jnp.int32, (width, width), 1), 1.0, 0.0)


def coefficients(sums, inv0, corner, inv1, factor_scale, width, col):
    scaled_eye = factor_scale * eye(width)
    down, turned = ((0,), (0,)), ((1,), (1,))
    cross0 = product(inv0, sums[:width])
    seen = jnp.where(col == 0, factor_scale * product(sums, inv0, turned), sums)
    cross1 = product(jnp.concatenate([corner, inv1], axis=1), seen)
    t1 = jnp.where(col == 1, -scaled_eye, jnp.where(col == 0, 0.0, cross1))
    t0 = jnp.where(col == 0, -scaled_eye, jnp.where(col == 1, 0.0, cross0))
    x1 = product(inv1, t1, down)
    x0 = product(inv0, t0, down) + product(corner, t1, down)
    return cross0, cross1, jnp.concatenate([x0, x1], axis=0)


def halves(a):
    high = a.astype(jnp.bfloat16)
    return high, (a - high.astype(jnp.float32)).astype(jnp.bfloat16)


def pieces(start, stop, size):
    return [(at, min(size, stop - at)) for at in range(start, stop, size)]


def kernel(
    n_row, n_x, n_z, late, factor_scale,
    matrix_ref, r_ref, out_ref,
    panels, mine, mixed, total, parts, theirs,
    late_rows, late_sums, late_parts, late_total, late_in, full, factors,
    load_sem, recv_sem, send_sem, extra_send, extra_recv, gather_send, gather_recv,
    scatter_send, scatter_recv, back_send, back_recv, swap_sem,
    rows_send, rows_recv, part_send, part_recv, late_send, late_recv,
):
    rows, width = mine.shape
    steps = rows // TILE
    early = steps - late
    half = steps // 2
    granule = GROUP * TILE
    row = lax.axis_index("row")
    col = lax.axis_index("col")
    x = lax.rem(col, n_x)
    z = col // n_x

    barrier = pltpu.get_barrier_semaphore()
    greeted = [
        (x > 0, col - 1), (x < n_x - 1, col + 1), (z > 0, col - n_x), (z < n_z - 1, col + n_x),
        (z > 1, x),
    ]
    greeted += [(z == 0, x + other * n_x) for other in range(2, n_z)]
    peers = n_row - 1
    for there, other in greeted:
        peers += jnp.where(there, 1, 0)

        @pl.when(there)
        def _():
            pl.semaphore_signal(barrier, inc=1, device_id={"col": other}, device_id_type=MESH)
    for step in range(1, n_row):
        peer = lax.rem(row + step, n_row)
        pl.semaphore_signal(barrier, inc=1, device_id={"row": peer}, device_id_type=MESH)
    load_mine = pltpu.make_async_copy(matrix_ref, mine, load_sem.at[0])
    load_mine.start()
    mixed[...] = jnp.zeros_like(mixed)
    pl.semaphore_wait(barrier, peers)

    def tile_at(index):
        return pl.ds(pl.multiple_of(index * TILE, TILE), TILE)

    def children(panel):
        return (
            (jnp.logical_and(x == panel, z < n_z - 1), col + n_x),
            (jnp.logical_and(x >= panel, x < n_x - 1), col + 1),
            (jnp.logical_and(x <= panel, x > 0), col - 1),
        )

    def forward(panel, index, source, which=(0, 1, 2)):
        for child, (there, other) in enumerate(children(panel)):
            if child not in which:
                continue

            @pl.when(there)
            def _():
                pltpu.make_async_remote_copy(
                    src_ref=source.at[tile_at(index)],
                    dst_ref=panels.at[panel, tile_at(index)],
                    send_sem=send_sem.at[panel, child],
                    recv_sem=recv_sem.at[panel, index],
                    device_id={"col": other},
                    device_id_type=MESH,
                ).start()

    def take(panel, index):
        here = panels.at[panel, tile_at(index)]
        pltpu.make_async_copy(here, here, recv_sem.at[panel, index]).wait()
        forward(panel, index, panels.at[panel])

    def place(panel, step):
        up = jnp.where(step < half + late, early - half, -late)
        down = jnp.where(step < late, early, jnp.where(step < half, half - late, -half))
        return step + jnp.where(panel == 1, down, jnp.where(step < half, 0, up))

    def both(at):
        return jnp.concatenate([panels[0, at], panels[1, at]], axis=1)

    def granule_at(index):
        return pl.ds(pl.multiple_of(index * granule, granule), granule)

    def cut(size, index):
        return pl.ds(pl.multiple_of(index * size, size), size)

    share = mixed.shape[0] // n_row
    third = width // n_row
    side = 3 * third // 2

    def row_copies(source, target, send, recv):
        copies = []
        for step in range(1, n_row):
            peer = lax.rem(row + step, n_row)
            copies.append(pltpu.make_async_remote_copy(
                src_ref=source(peer),
                dst_ref=target(step),
                send_sem=send.at[step - 1],
                recv_sem=recv.at[step - 1],
                device_id={"row": peer},
                device_id_type=MESH,
            ))
            copies[-1].start()
        return copies

    def scatter(source, size, turn):
        return row_copies(
            lambda peer: source(peer), lambda step: parts.at[turn, step - 1, pl.ds(0, size)],
            scatter_send.at[turn], scatter_recv.at[turn],
        )

    def settle(copies, source, size, turn, extra=None):
        summed = source(row)[...]
        if extra is not None:
            summed += extra()
        for step, copy in enumerate(copies):
            copy.wait_recv()
            summed += parts[turn, step, :size]
        here = total.at[turn, cut(size, row)]
        here[...] = summed
        return row_copies(
            lambda peer: here, lambda step: here, back_send.at[turn], back_recv.at[turn]
        )

    def mixed_part(peer):
        return mixed.at[cut(share, peer)]

    def extra_part(panel):
        return factors.at[row, pl.ds(pl.multiple_of(panel * side, side), side)]

    def forward_extra(panel):
        for child, (there, other) in enumerate(children(panel)):
            @pl.when(there)
            def _():
                pltpu.make_async_remote_copy(
                    src_ref=extra_part(panel),
                    dst_ref=extra_part(panel),
                    send_sem=extra_send.at[panel, child],
                    recv_sem=extra_recv.at[panel],
                    device_id={"col": other},
                    device_id_type=MESH,
                ).start()

    def take_extra(panel):
        here = extra_part(panel)
        pltpu.make_async_copy(here, here, extra_recv.at[panel]).wait()
        forward_extra(panel)

    def gather_factors():
        here = factors.at[row]
        return row_copies(lambda peer: here, lambda step: here, gather_send, gather_recv)

    def read_factors():
        return [
            jnp.concatenate(
                [factors[part, kind * third:(kind + 1) * third] for part in range(n_row)], axis=0
            )
            for kind in range(3)
        ]

    def solve(sums, inv0, corner, inv1):
        cross0, cross1, mix = coefficients(sums, inv0, corner, inv1, factor_scale, width, col)
        r_ref[0] = cross0 / factor_scale
        r_ref[1] = cross1 / factor_scale
        mix_high, mix_low = halves(mix)
        return mix_high, jnp.concatenate([mix_high, mix_low], axis=1)

    def update(mix, start, size):
        mix_high, mix_both = mix
        at = pl.ds(start, size)
        high, low = halves(both(at))
        main = jnp.dot(high, mix_both, preferred_element_type=jnp.float32)
        rest = jnp.dot(low, mix_high, preferred_element_type=jnp.float32)
        removed = main[:, :width] + (main[:, width:] + rest)
        out_ref[at] = jnp.where(col >= PANELS, mine[at], 0.0) - removed

    def sum_late(block):
        here = late_rows.at[block]
        pltpu.make_async_copy(here, here, rows_recv.at[block]).wait()
        late_sums[block] = jnp.zeros_like(late_sums[block])

        @pl.loop(0, late * TILE // DEEP)
        def _(index):
            at = pl.ds(pl.multiple_of(early * TILE + index * DEEP, DEEP), DEEP)
            late_sums[block] += outer(both(at), late_rows[block, cut(DEEP, index)])

    def scatter_late():
        return row_copies(
            lambda peer: late_sums.at[:, cut(share, peer)], lambda step: late_parts.at[step - 1],
            part_send, part_recv,
        )

    def late_copies():
        return [
            pltpu.make_async_remote_copy(
                src_ref=late_total.at[block],
                dst_ref=late_in,
                send_sem=late_send.at[block],
                recv_sem=late_recv,
                device_id={"col": x + (block + 1) * n_x},
                device_id_type=MESH,
            )
            for block in range(n_z - 1)
        ]

    def send_late(copies):
        summed = late_sums[:, cut(share, row)]
        for step, copy in enumerate(copies):
            copy.wait_recv()
            summed += late_parts[step]
        late_total[...] = summed
        sends = late_copies()
        for copy in sends:
            copy.start()
        return sends

    def finish_sends(copies):
        for copy in copies:
            copy.wait_send()

    def finish(copies):
        for copy in copies:
            copy.wait_recv()

    @pl.when(col < PANELS)
    def _():
        second = 1 - col
        first = col == 0

        @pl.loop(0, early)
        def _(index):
            forward(col, index, matrix_ref, (0,))

        @pl.loop(0, FIRST)
        def _(step):
            forward(col, place(col, step), matrix_ref, (1, 2))

        load_mine.wait()
        own = pltpu.make_async_copy(mine, panels.at[col], load_sem.at[1])
        own.start()
        block = pl.ds(pl.multiple_of(col * width, width), width)
        other_block = pl.ds(pl.multiple_of(second * width, width), width)

        def block_part(panel):
            def part(peer):
                start = panel * width + peer * third
                return mixed.at[pl.ds(pl.multiple_of(start, third), third)]
            return part

        def swap(turn):
            copy = pltpu.make_async_remote_copy(
                src_ref=total.at[turn, pl.ds(0, width)],
                dst_ref=theirs.at[turn],
                send_sem=swap_sem.at[turn, 0],
                recv_sem=swap_sem.at[turn, 1],
                device_id={"col": 1 - col},
                device_id_type=MESH,
            )
            copy.start()
            return copy

        @pl.loop(0, rows // granule)
        def _(index):
            at = granule_at(index)
            mixed[block] += outer(mine[at], mine[at])

        copies = scatter(block_part(col), third, 0)
        backs = settle(copies, block_part(col), third, 0)
        finish(backs)
        sent = copies + backs
        grams = swap(0)

        @pl.loop(FIRST, half + AHEAD)
        def _(step):
            forward(col, place(col, step), matrix_ref, (1, 2))

        grams.wait()
        gram0 = jnp.where(first, total[0, :width], theirs[0])
        full[0] = inverse_factor(gram0)
        own.wait()

        @pl.loop(0, half // GROUP)
        def _(group):
            for step in range(GROUP):
                take(second, place(second, group * GROUP + step))
            at = granule_at(place(second, group * GROUP) // GROUP)
            mixed[other_block] += outer(panels[second, at], mine[at])

        copies = scatter(block_part(second), third, 1)
        backs = settle(copies, block_part(second), third, 1)
        finish(backs)
        sent += copies + backs
        crossed = swap(1)

        @pl.loop(half + AHEAD, steps)
        def _(step):
            forward(col, place(col, step), matrix_ref, (1, 2))

        crossed.wait()
        inv0 = full[0]
        gram0 = jnp.where(first, total[0, :width], theirs[0])
        gram1 = jnp.where(first, theirs[0], total[0, :width])
        ours, other = total[1, :width], theirs[1]
        gram01 = jnp.where(first, ours.T + other, ours + other.T)
        r01 = product(inv0, gram01)
        inv1 = inverse_factor(gram1 - product(r01, r01, ((0,), (0,))))
        corner = -product(product(inv1, r01, ((1,), (1,))), inv0)
        full[1], full[2] = corner, inv1
        whole = jnp.concatenate([full[kind, cut(third, row)] for kind in range(3)], axis=0)
        extra_part(col)[...] = jnp.where(first, whole[:side], whole[side:])
        forward_extra(col)

        @pl.loop(early, early + HOLD)
        def _(index):
            forward(col, index, matrix_ref, (0,))

        @pl.loop(half, half + late)
        def _(step):
            take(second, place(second, step))

        for number in reversed(range(n_z - 1)):
            sum_late(number)
        late_scatter = scatter_late()
        late_sends = send_late(late_scatter)

        @pl.loop(early + HOLD, steps)
        def _(index):
            forward(col, index, matrix_ref, (0,))

        sums = jnp.concatenate(
            [jnp.where(first, gram0, gram01), jnp.where(first, gram01.T, gram1)], axis=0
        )
        mix = solve(sums, inv0, corner, inv1)

        def renew(group):
            start = place(second, group * BATCH) * TILE
            update(mix, pl.multiple_of(start, BATCH * TILE), BATCH * TILE)

        @pl.loop(0, (half + late) // BATCH)
        def _(group):
            renew(group)

        @pl.loop((half + late) // BATCH, steps // BATCH)
        def _(group):
            for step in range(BATCH):
                take(second, place(second, group * BATCH + step))
            renew(group)

        take_extra(second)
        finish_sends(late_scatter + late_sends + sent)

    @pl.when(z > 0)
    def _():
        main = jnp.where(x == 1, 1, 0)
        second = 1 - main
        last = pl.ds(early * TILE, late * TILE)
        for block in range(n_z - 1):
            @pl.when(z == block + 1)
            def _():
                pltpu.make_async_remote_copy(
                    src_ref=matrix_ref.at[last],
                    dst_ref=late_rows.at[block],
                    send_sem=rows_send,
                    recv_sem=rows_recv.at[block],
                    device_id={"col": x},
                    device_id_type=MESH,
                ).start()
        load_mine.wait()

        def add(index):
            at = granule_at(index)
            mixed[...] += outer(both(at), mine[at])

        def slot(index):
            take(main, index)
            take(second, index - LAG)

        behind = LAG // GROUP

        @pl.loop(0, LAG)
        def _(index):
            take(main, index)

        @pl.loop(behind, early // GROUP)
        def _(group):
            for step in range(GROUP):
                slot(group * GROUP + step)
            add(group - behind)

        spot = [early]

        def slots(count):
            stop = min(spot[0] + count, steps)

            @pl.loop(spot[0], stop)
            def _(index):
                slot(index)
            spot[0] = stop

        take_extra(main)
        slots(LAG)
        take_extra(second)
        gathers = gather_factors()

        @pl.loop(early // GROUP - behind, early // GROUP)
        def _(group):
            add(group)

        copies = scatter(mixed_part, share, 0)
        slots(6)

        def brought():
            pltpu.make_async_copy(late_in, late_in, late_recv).wait()
            return late_in[...]

        backs = settle(copies, mixed_part, share, 0, brought)
        slots(6)
        finish(gathers)
        inverses = read_factors()
        finish(backs)
        mix = solve(total[0], *inverses)
        work = pieces(0, early * TILE, CHUNK)
        left_over = steps - spot[0]
        for number, (start, size) in enumerate(work):
            update(mix, start, size)
            slots(left_over * (number + 1) // (2 * len(work)) - (spot[0] - steps + left_over))
        reach = early * TILE
        for start, size in pieces(reach, rows, 2 * granule):
            need = (start + size) // TILE
            if need == steps:
                break
            slots(max(0, min(need + LAG, steps) - spot[0]))
            update(mix, start, size)
            reach = start + size
        slots(steps - spot[0])

        @pl.loop(steps - LAG, steps)
        def _(index):
            take(second, index)

        update(mix, reach, rows - reach)
        finish_sends(copies + backs + gathers)
        pltpu.make_async_remote_copy(
            src_ref=matrix_ref.at[last],
            dst_ref=late_rows.at[0],
            send_sem=rows_send,
            recv_sem=rows_recv.at[0],
            device_id={"col": x},
            device_id_type=MESH,
        ).wait_send()

    if n_x > PANELS:
        @pl.when(jnp.logical_and(z == 0, col >= PANELS))
        def _():
            load_mine.wait()

            @pl.loop(0, steps)
            def _(step):
                take(0, place(0, step))
                take(1, place(1, step))

            for block in range(n_z - 1):
                sum_late(block)
            late_scatter = scatter_late()
            late_sends = send_late(late_scatter)

            @pl.loop(0, rows // granule)
            def _(index):
                at = granule_at(index)
                mixed[...] += outer(both(at), mine[at])

            take_extra(0)
            take_extra(1)
            gathers = gather_factors()
            copies = scatter(mixed_part, share, 0)
            backs = settle(copies, mixed_part, share, 0)
            finish(gathers)
            inverses = read_factors()
            finish(backs)
            mix = solve(total[0], *inverses)

            @pl.loop(0, rows // CHUNK)
            def _(index):
                update(mix, pl.multiple_of(index * CHUNK, CHUNK), CHUNK)

            finish_sends(late_scatter + late_sends + copies + backs + gathers)

    for panel in range(PANELS):
        for child, (there, other) in enumerate(children(panel)):
            @pl.when(there)
            def _():
                pltpu.make_async_remote_copy(
                    src_ref=panels.at[panel],
                    dst_ref=panels.at[panel],
                    send_sem=send_sem.at[panel, child],
                    recv_sem=recv_sem.at[panel, 0],
                    device_id={"col": other},
                    device_id_type=MESH,
                ).wait_send()
                pltpu.make_async_remote_copy(
                    src_ref=extra_part(panel),
                    dst_ref=extra_part(panel),
                    send_sem=extra_send.at[panel, child],
                    recv_sem=extra_recv.at[panel],
                    device_id={"col": other},
                    device_id_type=MESH,
                ).wait_send()


def solution(mesh):
    n_row, n_col = mesh.shape["row"], mesh.shape["col"]
    n_x = max(PANELS, n_row // 2)
    n_z = n_col // n_x
    assert n_x * n_z == n_col and n_z > 1

    def local(matrix):
        rows, width = matrix.shape
        steps = rows // TILE
        late = LATE
        assert rows % CHUNK == 0 and late * TILE % DEEP == 0
        assert late % BATCH == 0 and steps % (2 * BATCH) == 0 and late < steps // 2
        deep = PANELS * width
        share, third = deep // n_row, width // n_row
        vmem = pltpu.VMEM
        f32 = jnp.float32
        dma = pltpu.SemaphoreType.DMA
        in_vmem = pl.BlockSpec(memory_space=vmem)
        return pl.pallas_call(
            functools.partial(kernel, n_row, n_x, n_z, late, math.sqrt(rows * n_row)),
            out_shape=(
                jax.ShapeDtypeStruct((PANELS, width, width), f32),
                jax.ShapeDtypeStruct((rows, width), f32),
            ),
            in_specs=[pl.BlockSpec(memory_space=pl.ANY)],
            out_specs=(in_vmem, in_vmem),
            scratch_shapes=[
                vmem((PANELS, rows, width), f32),
                vmem((rows, width), f32),
                vmem((deep, width), f32),
                vmem((2, deep, width), f32),
                vmem((2, n_row - 1, share, width), f32),
                vmem((2, width, width), f32),
                vmem((n_z - 1, late * TILE, width), f32),
                vmem((n_z - 1, deep, width), f32),
                vmem((n_row - 1, n_z - 1, share, width), f32),
                vmem((n_z - 1, share, width), f32),
                vmem((share, width), f32),
                vmem((3, width, width), f32),
                vmem((n_row, 3 * third, width), f32),
                dma((2,)),
                dma((PANELS, steps)),
                dma((PANELS, 3)),
                dma((PANELS, 3)),
                dma((PANELS,)),
                dma((n_row - 1,)),
                dma((n_row - 1,)),
                dma((2, n_row - 1)),
                dma((2, n_row - 1)),
                dma((2, n_row - 1)),
                dma((2, n_row - 1)),
                dma((2, 2)),
                dma,
                dma((n_z - 1,)),
                dma((n_row - 1,)),
                dma((n_row - 1,)),
                dma((n_z - 1,)),
                dma,
            ],
            compiler_params=pltpu.CompilerParams(
                collective_id=0, has_side_effects=True, vmem_limit_bytes=47 * 1024 * 1024
            ),
        )(matrix)

    return jax.shard_map(
        local,
        mesh=mesh,
        in_specs=(P("row", "col"),),
        out_specs=(P(None, None, "col"), P("row", "col")),
        check_vma=False,
    )
```
